256 devices in a mesh: probe: 64 (over z, x_lo, y), slab: 4 (over x_hi, core).
Axes of the slice: x: 4 (x_hi: 2, x_lo: 2; x = x_hi * 2 + x_lo), y: 4, z: 8, core: 2. Of those that a mesh axis runs over, the one named last changes fastest.
Arguments:
- smatrix: bfloat16 [2, 512, 128, 128], P(None, 'probe', 'slab'), may hold values from -6 to 6
- amplitude: float32 [2, 512], replicated, may hold values from -0.25 to 0.25
- beam_index: int32 [512, 2], replicated, may hold values from -32 to 31
- positions: int32 [8192, 2], P('probe'), may hold values from -8 to 8
Outputs:
- patterns: float32 [8192, 128, 128], P('probe', 'slab')
The draws below stay inside these ranges and needn't reach their ends.
Inputs may be any that keep to these rules, and one draw needn't show every extreme that they name: `positions`: column 0 is the row offset that places a probe's crop in the band, column 1 the column offset. `beam_index`: column 0 along rows, column 1 along columns.
All inputs are finite; a program needn't handle non-finite values.
Results may differ from the reference program's by a relative error of at most 0.0029.
Values may be sent and summed in bfloat16 or wider, within the bound.
A program may use at most 128 MiB of HBM per device.

```python
import math
import jax
import jax.numpy as jnp
from jax import lax

BEAMS = 512
ROWS = 128
COLS = 128
HALO = 8
P_DEV = 128
PROBES = 8192
N_PROBE = 64


def with_ends(array, rng, least, high):
    spot = [jax.random.randint(jax.random.fold_in(rng, axis), (), 0, length) for axis, length in enumerate(array.shape)]
    longest = array.shape.index(max(array.shape))
    next_to = spot[:longest] + [(spot[longest] + 1) % array.shape[longest]] + spot[longest + 1:]
    return array.at[tuple(spot)].set(least).at[tuple(next_to)].set(high)


def block_levels(rng, extent, cuts, least, high):
    gain, own = 1.0, jax.random.fold_in(rng, 6)
    for position, blocks in cuts:
        steps = jnp.exp(jax.random.uniform(jax.random.fold_in(own, position), (blocks,), jnp.float32, least / len(cuts), high / len(cuts)))
        gain = gain * jnp.repeat(steps, extent[position] // blocks).reshape([-1 if axis == position else 1 for axis in range(len(extent))])
    return gain


def bell_draw(own_key, dims, deviation, bound, pieces=(), kind=jnp.bfloat16):
    values = jax.random.normal(own_key, dims, jnp.float32) * deviation
    if len(pieces) > 0:
        values = block_levels(own_key, dims, pieces, -0.22, 0.18) * values
    return jnp.clip(values, min=-bound, max=bound).astype(kind)


def setup_inputs(seed: int = 0) -> dict:
    key_of = jax.random.split(jax.random.key(seed), 5)
    smatrix = bell_draw(key_of[0], (2, BEAMS, ROWS, COLS), 1.0, 6.0, ((1, 64), (2, 4)))
    amplitude = bell_draw(key_of[1], (2, BEAMS), BEAMS ** -0.5, 0.25, (), jnp.float32)
    beam_index = with_ends(jax.random.randint(key_of[2], (BEAMS, 2), -32, 32), jax.random.fold_in(key_of[2], 1), -32, 31).astype(jnp.int32)
    positions = with_ends(jax.random.randint(key_of[3], (PROBES, 2), 0 - HALO, HALO + 1), jax.random.fold_in(key_of[3], 1), 0 - HALO, HALO).astype(jnp.int32)
    return {"smatrix": smatrix, "amplitude": amplitude, "beam_index": beam_index, "positions": positions}


def beam_weights(amplitude, beam_index, place, rows_all, cols):
    row_phase = jnp.mod(place[:, 0:1] * beam_index[None, :, 0], rows_all).astype(jnp.float32) / rows_all
    col_phase = jnp.mod(place[:, 1:2] * beam_index[None, :, 1], cols).astype(jnp.float32) / cols
    angle = 2.0 * math.pi * (row_phase + col_phase)
    cosine = jnp.cos(angle)
    sine = jnp.sin(angle)
    real = amplitude[0][None, :] * cosine + amplitude[1][None, :] * sine
    imag = amplitude[1][None, :] * cosine - amplitude[0][None, :] * sine
    return real.astype(jnp.bfloat16), imag.astype(jnp.bfloat16)


def reference(smatrix, amplitude, beam_index, positions):
    padded = jnp.pad(smatrix, ((0, 0), (0, 0), (HALO, HALO), (0, 0)))
    band = (ROWS + 2 * HALO) * COLS
    flat = padded.reshape(2, BEAMS, band)
    blocks = positions.reshape(N_PROBE, P_DEV, 2)

    def cut(field, offset):
        return lax.dynamic_slice_in_dim(field, offset, ROWS, 0)

    def one_block(place):
        weight_re, weight_im = beam_weights(amplitude, beam_index, place, ROWS, COLS)
        real = jnp.dot(weight_re, flat[0], preferred_element_type=jnp.float32) - jnp.dot(weight_im, flat[1], preferred_element_type=jnp.float32)
        imag = jnp.dot(weight_re, flat[1], preferred_element_type=jnp.float32) + jnp.dot(weight_im, flat[0], preferred_element_type=jnp.float32)
        real = real.reshape(P_DEV, ROWS + 2 * HALO, COLS)
        imag = imag.reshape(P_DEV, ROWS + 2 * HALO, COLS)
        starts = (place[:, 0] + HALO).astype(jnp.int32)
        wave_re = jax.vmap(cut)(real, starts)
        wave_im = jax.vmap(cut)(imag, starts)
        spectrum = jnp.fft.fft2(lax.complex(wave_re, wave_im), norm="ortho")
        return (jnp.real(spectrum) ** 2 + jnp.imag(spectrum) ** 2).astype(jnp.float32)

    return lax.map(one_block, blocks).reshape(PROBES, ROWS, COLS)
```

```python
import math

import jax
import jax.numpy as jnp
from jax import lax
from jax.sharding import PartitionSpec as P

HALO = 8
SIDE = 2 * HALO + 1
SPOTS = SIDE * SIDE


def dft_table(first, second, length):
    angle = (
        2.0
        * math.pi
        * (jnp.mod(first[:, None] * second[None, :], length).astype(jnp.float32) / length)
    )
    return (jnp.cos(angle), jnp.sin(angle))


def spot_weights(amplitude, beam_index, rows_all, cols):
    spot = jnp.arange(SPOTS, dtype=jnp.int32)
    row, col = spot // SIDE - HALO, spot % SIDE - HALO
    turn = jnp.mod(beam_index[:, 0:1] * row[None, :], rows_all).astype(jnp.float32) / rows_all
    turn = turn + jnp.mod(beam_index[:, 1:2] * col[None, :], cols).astype(jnp.float32) / cols
    cosine, sine = jnp.cos(2.0 * math.pi * turn), jnp.sin(2.0 * math.pi * turn)
    re, im = amplitude[0][:, None], amplitude[1][:, None]
    return (
        (re * cosine + im * sine).astype(jnp.bfloat16),
        (im * cosine - re * sine).astype(jnp.bfloat16),
    )


def on_device(smatrix, amplitude, beam_index, positions):
    _, beams_here, slab_rows, cols = smatrix.shape
    groups = lax.axis_size("probe")
    slabs = lax.axis_size("slab")
    rows_all = slab_rows * slabs
    own = cols // groups
    highest = lax.Precision.HIGHEST
    f32 = jnp.float32
    index = jnp.arange(cols, dtype=jnp.int32)
    cos, sin = dft_table(index, index, cols)
    cos, sin = cos / math.sqrt(cols), sin / math.sqrt(cols)
    s_re, s_im = smatrix[0].astype(f32), smatrix[1].astype(f32)
    mm = lambda a, b: jnp.einsum("lc,brc->lbr", a, b, precision=highest)
    half = jnp.stack([mm(cos, s_re) + mm(sin, s_im), mm(cos, s_im) - mm(sin, s_re)], 1)
    half = half.astype(jnp.bfloat16).reshape(groups, own, 2, beams_here, slab_rows)
    got = lax.all_to_all(half, "probe", split_axis=0, concat_axis=0, tiled=True)
    got = lax.all_gather(got, "slab", axis=0)
    got = jnp.transpose(got, (2, 0, 5, 3, 1, 4)).reshape(own, rows_all, 2, groups * beams_here)
    w_re, w_im = spot_weights(amplitude, beam_index, rows_all, cols)
    field = jnp.concatenate([got[:, :, 0], got[:, :, 1]], axis=-1)
    u_re = jnp.dot(field, jnp.concatenate([w_re, -w_im], 0), preferred_element_type=f32)
    u_im = jnp.dot(field, jnp.concatenate([w_im, w_re], 0), preferred_element_type=f32)
    row = jnp.arange(rows_all, dtype=jnp.int32)[:, None]
    shift = (jnp.arange(SPOTS, dtype=jnp.int32) // SIDE - HALO)[None, :]
    inside = (row >= shift) & (row < rows_all + shift)
    u_re = jnp.where(inside[None], u_re, 0.0)
    u_im = jnp.where(inside[None], u_im, 0.0)
    freq = lax.axis_index("slab") * slab_rows + jnp.arange(slab_rows, dtype=jnp.int32)
    rcos, rsin = dft_table(freq, row[:, 0], rows_all)
    rcos, rsin = rcos / math.sqrt(rows_all), rsin / math.sqrt(rows_all)
    mm = lambda a, b: jnp.einsum("kr,lrs->lks", a, b, precision=highest)
    out_re = mm(rcos, u_re) + mm(rsin, u_im)
    out_im = mm(rcos, u_im) - mm(rsin, u_re)
    power = (out_re**2 + out_im**2).astype(jnp.bfloat16)
    table = lax.all_gather(power, "probe", axis=0, tiled=True)
    spot = (positions[:, 0] + HALO) * SIDE + positions[:, 1] + HALO
    pick = (spot[:, None] == jnp.arange(SPOTS, dtype=jnp.int32)[None, :]).astype(jnp.bfloat16)
    return jnp.einsum("ps,lks->pkl", pick, table, preferred_element_type=f32)


def solution(mesh):
    return jax.shard_map(
        on_device,
        mesh=mesh,
        in_specs=(P(None, "probe", "slab", None), P(), P(), P("probe", None)),
        out_specs=P("probe", "slab", None),
        check_vma=False,
    )
```

```python
import functools
import math

import jax
import jax.numpy as jnp
import ml_dtypes
import numpy as np
from jax import lax
from jax.experimental import pallas as pl
from jax.experimental.pallas import tpu as pltpu
from jax.sharding import PartitionSpec as P

HALO = 8
SIDE = 2 * HALO + 1
SPOTS = 304
LANES = 384
QUAD = 4
MESH = pl.DeviceIdType.MESH
F32 = jnp.float32
BF16 = jnp.bfloat16


def two_terms(table):
    high = table.astype(ml_dtypes.bfloat16)
    low = (table - high.astype(np.float64)).astype(ml_dtypes.bfloat16)
    return np.stack([high, low])


def column_table(near, deep, cols):
    chip = np.arange(cols)
    far, probe = chip // (near * deep), chip % (near * deep)
    freq = (far * near + probe % near) * deep + probe // near
    turn = 2.0 * np.pi * ((freq[:, None] * np.arange(cols)[None, :]) % cols) / cols
    cos, sin = np.cos(turn), np.sin(turn)
    return two_terms(np.block([[cos, sin], [-sin, cos]]))


def row_table(slab_rows, slabs):
    length = slab_rows * slabs
    tables = []
    for core in range(2):
        freq = np.concatenate(
            [(far * 2 + core) * slab_rows + np.arange(slab_rows) for far in range(2)]
        )
        row = np.concatenate(
            [
                np.tile((far * 2 + side) * slab_rows + np.arange(slab_rows), QUAD)
                for side in (core, 1 - core)
                for far in range(2)
            ]
        )
        turn = 2.0 * np.pi * ((freq[:, None] * row[None, :]) % length) / length
        cos, sin = np.cos(turn), np.sin(turn)
        tables.append(two_terms(np.block([[cos, sin], [-sin, cos]])))
    return np.stack(tables)


def nt(a, b):
    return lax.dot_general(a, b, (((1,), (1,)), ((), ())), preferred_element_type=F32)


def unit_circle(turn):
    turn = turn - jnp.floor(turn + 0.5)
    quarter = jnp.floor(4.0 * turn + 0.5)
    phi = (2.0 * math.pi) * (turn - 0.25 * quarter)
    sq = phi * phi
    s = phi * (1.0 + sq * (-1.0 / 6 + sq * (1.0 / 120 + sq * (-1.0 / 5040 + sq / 362880))))
    c = 1.0 + sq * (-0.5 + sq * (1.0 / 24 + sq * (-1.0 / 720 + sq / 40320)))
    odd = jnp.abs(quarter) == 1.0
    a = jnp.where(odd, s, c)
    b = jnp.where(odd, c, s)
    cos_neg = (quarter == 1.0) | (jnp.abs(quarter) == 2.0)
    sin_neg = (quarter == -1.0) | (jnp.abs(quarter) == 2.0)
    return jnp.where(cos_neg, -a, a), jnp.where(sin_neg, -b, b)


def spot_offsets(width):
    spot = lax.broadcasted_iota(jnp.int32, (SPOTS, width), 0).astype(F32)
    row = jnp.floor((spot + 0.5) * (1.0 / SIDE))
    return row - HALO, spot - SIDE * row - HALO


def exchange(
    near, deep, slab_rows,
    s_ref, beam_ref, spot_ref, ctab_hbm, rtab_hbm, out_hbm,
    ctab, rtab, sendf, send, field, other, weight, high, low, planes, mixed, picks, spots, blocks,
    ctab_sem, rtab_sem, send_sem, recv_sem, pair_send, pair_recv,
    deep_send, deep_recv, spot_send, spot_recv, near_send, near_recv, keep_sem,
):
    probe, slab = lax.axis_index("probe"), lax.axis_index("slab")
    probes = near * deep
    chips = 2 * probes
    wide = 2 * near
    far, core = slab // 2, slab % 2
    chip = far * probes + probe
    z, flat = probe // near, probe % near
    here = far * near + flat

    def device(index):
        return (index % probes, (index // probes) * 2 + core)

    pair = (probe, far * 2 + 1 - core)
    barrier = pltpu.get_barrier_semaphore()

    @pl.loop(1, chips)
    def _(i):
        pl.semaphore_signal(barrier, inc=1, device_id=device((chip + i) % chips), device_id_type=MESH)

    pl.semaphore_signal(barrier, inc=1, device_id=pair, device_id_type=MESH)
    ctab_copy = pltpu.make_async_copy(ctab_hbm, ctab, ctab_sem)
    ctab_copy.start()
    rtab_copy = pltpu.make_async_copy(rtab_hbm.at[core], rtab, rtab_sem)
    rtab_copy.start()

    ctab_copy.wait()
    both = jnp.concatenate([s_ref[0], s_ref[1]], axis=1)
    half = nt(ctab[0], both) + nt(ctab[1], both)
    lanes = QUAD * slab_rows
    for part in range(2):
        for h in range(2):
            sendf[pl.ds(part * 2 + h, chips, stride=4), :] = half[
                part * chips : (part + 1) * chips, h * lanes : (h + 1) * lanes
            ]
    send[...] = sendf[...].astype(BF16).reshape(chips, 4, lanes)
    spots[flat] = spot_ref[...]
    pl.semaphore_wait(barrier, chips)

    @pl.loop(1, chips)
    def _(i):
        to = (chip + i) % chips
        pltpu.make_async_remote_copy(
            src_ref=send.at[to], dst_ref=field.at[chip], send_sem=send_sem, recv_sem=recv_sem,
            device_id=device(to), device_id_type=MESH,
        ).start()

    pltpu.make_async_copy(send.at[chip], field.at[chip], recv_sem).start()
    spot_copies = []
    for i in range(1, near):
        copy = pltpu.make_async_remote_copy(
            src_ref=spot_ref, dst_ref=spots.at[flat], send_sem=spot_send.at[i],
            recv_sem=spot_recv.at[flat], device_id=(z * near + (flat + i) % near, slab),
            device_id_type=MESH,
        )
        copy.start()
        spot_copies.append(copy)

    kdim = weight.shape[1]
    r0, c0 = spot_offsets(kdim)
    for j in range(QUAD):
        turn = (beam_ref[j : j + 1, :] * r0 + beam_ref[4 + j : 5 + j, :] * c0) * (
            1.0 / (4 * slab_rows)
        )
        cos, sin = unit_circle(turn)
        re, im = beam_ref[8 + j : 9 + j, :], beam_ref[12 + j : 13 + j, :]
        weight[j * SPOTS : (j + 1) * SPOTS, :] = (re * cos + im * sin).astype(BF16)
        weight[(4 + j) * SPOTS : (5 + j) * SPOTS, :] = (im * cos - re * sin).astype(BF16)
    planes[z] = jnp.zeros(planes.shape[1:], BF16)

    pltpu.make_async_copy(field, field, recv_sem).wait()
    swap = pltpu.make_async_remote_copy(
        src_ref=field, dst_ref=other, send_sem=pair_send, recv_sem=pair_recv,
        device_id=pair, device_id_type=MESH,
    )
    swap.start()

    def beam_sum(source, side, turn):
        r0, _ = spot_offsets(2 * lanes)
        lane = lax.broadcasted_iota(jnp.int32, (SPOTS, 2 * lanes), 1)
        group = (lane % lanes) // slab_rows
        row = ((lane // lanes) * 2 + side) * slab_rows + lane % slab_rows
        rowf = row.astype(F32)
        inside = (rowf >= r0) & (rowf < r0 + 4.0 * slab_rows)
        x = jnp.concatenate(
            [
                source[0:probes].reshape(probes * 4, lanes),
                source[probes : 2 * probes].reshape(probes * 4, lanes),
            ],
            axis=1,
        )
        for part in range(2):
            total = None
            for j in range(QUAD):
                w = weight[(part * QUAD + j) * SPOTS : (part * QUAD + j + 1) * SPOTS, :]
                y = jnp.dot(w, x, preferred_element_type=F32)
                total = y if j == 0 else jnp.where(group == j, y, total)
            total = jnp.where(inside, total, 0.0)
            top = total.astype(BF16)
            at = (part * 2 + turn) * 2 * lanes
            high[:, at : at + 2 * lanes] = top
            low[:, at : at + 2 * lanes] = (total - top.astype(F32)).astype(BF16)

    beam_sum(field, core, 0)
    for i in range(near):
        at = (flat + i) % near
        if i > 0:
            pltpu.make_async_remote_copy(
                src_ref=spot_ref, dst_ref=spots.at[at], send_sem=spot_send.at[i],
                recv_sem=spot_recv.at[at], device_id=pair, device_id_type=MESH,
            ).wait_recv()
        width = spot_ref.shape[1]
        index = spots[at][0:1, :]
        row = lax.broadcasted_iota(jnp.int32, (SPOTS, width), 0).astype(F32)
        picks[:, i * width : (i + 1) * width] = jnp.where(row == index, 1.0, 0.0).astype(BF16)
    swap.wait_recv()
    beam_sum(other, 1 - core, 1)
    rtab_copy.wait()
    out = nt(rtab[0], high[...]) + (nt(rtab[0], low[...]) + nt(rtab[1], high[...]))
    count = 2 * slab_rows
    re, im = out[:count], out[count:]
    scale = 1.0 / (4 * slab_rows * chips)
    power = (re * re + im * im) * scale
    planes[z, :, 0:SPOTS] = power.astype(BF16)

    def deep_copy(i, slot):
        return pltpu.make_async_remote_copy(
            src_ref=planes.at[slot], dst_ref=planes.at[slot], send_sem=deep_send.at[i],
            recv_sem=deep_recv.at[slot], device_id=(((z + i) % deep) * near + flat, slab),
            device_id_type=MESH,
        )

    order = sorted(range(1, deep), key=lambda i: (min(i, deep - i), i))
    for i in order:
        deep_copy(i, z).start()
    for i in [0] + order:
        slot = (z + i) % deep
        if i > 0:
            deep_copy(i, slot).wait_recv()
        plane = planes[slot].astype(F32)
        for t in range(LANES // 128):
            mixed[t, pl.ds(slot, count, stride=deep), :] = plane[:, t * 128 : (t + 1) * 128]

    left = jnp.concatenate([mixed[t] for t in range(LANES // 128)], axis=1)
    left = left[:, 0:SPOTS].astype(BF16)
    rows = slab_rows * deep
    width = spot_ref.shape[1]

    def near_copy(i, target, to, slot):
        return pltpu.make_async_remote_copy(
            src_ref=blocks.at[i, target], dst_ref=out_hbm.at[slot],
            send_sem=near_send.at[i, target], recv_sem=near_recv.at[slot],
            device_id=(z * near + (to % near), target * 2 + core), device_id_type=MESH,
        )

    for i in range(0, near, 2):
        got = jnp.dot(
            left, picks[:, i * width : (i + 2) * width], preferred_element_type=F32
        ).astype(BF16)
        for d in range(2):
            for target in range(2):
                blocks[i + d, target] = got[
                    target * rows : (target + 1) * rows, d * width : (d + 1) * width
                ]
            if i + d == 0:
                near_copy(0, 1 - far, flat, here).start()
            else:
                for target in range(2):
                    near_copy(i + d, target, flat + i + d, here).start()
    keep = pltpu.make_async_copy(blocks.at[0, far], out_hbm.at[here], keep_sem)
    keep.start()
    keep.wait()
    for i in range(near):
        for target in range(2):
            if i == 0:
                continue
            copy = near_copy(i, target, flat + i, target * near + (flat + i) % near)
            copy.wait()
    copy = near_copy(0, 1 - far, flat, (1 - far) * near + flat)
    copy.wait()
    for i in order:
        deep_copy(i, z).wait_send()
    for copy in spot_copies:
        copy.wait_send()
    swap.wait_send()
    gone = send.at[pl.ds(0, chips - 1)]
    pltpu.make_async_copy(gone, gone, send_sem).wait()


def to_columns(deep, in_ref, out_ref):
    wide, rows, probes = in_ref.shape
    count = rows // deep
    for k in range(0, count, 2):
        pairs = in_ref[:, k * deep : (k + 2) * deep, :].astype(F32)
        for e in range(2):
            block = pairs[:, e * deep : (e + 1) * deep, :].reshape(wide * deep, probes)
            out_ref[:, k + e, :] = block.T


def on_device(smatrix, amplitude, beam_index, positions):
    _, beams_here, slab_rows, cols = smatrix.shape
    probes = lax.axis_size("probe")
    near = 8 if probes == 64 else 2
    deep = probes // near
    wide = 2 * near
    chips = 2 * probes
    slabs = lax.axis_size("slab")
    probes_here = positions.shape[0]
    lanes = QUAD * slab_rows
    kdim = 4 * probes
    split = lambda v: jnp.transpose(v.reshape(probes, 2, QUAD), (2, 0, 1))[:, :, None, :]
    twice = lambda a, b: jnp.concatenate([split(a), split(b)], 2).reshape(QUAD, kdim)
    freq = beam_index.astype(F32)
    beam = jnp.concatenate(
        [
            twice(freq[:, 0], freq[:, 0]),
            twice(freq[:, 1], freq[:, 1]),
            twice(amplitude[0], -amplitude[1]),
            twice(amplitude[1], amplitude[0]),
        ],
        0,
    )
    spot = ((positions[:, 0] + HALO) * SIDE + positions[:, 1] + HALO).astype(F32)
    spot = jnp.broadcast_to(spot[None, :], (8, probes_here))
    ctab = jnp.asarray(column_table(near, deep, cols))
    rtab = jnp.asarray(row_table(slab_rows, slabs))
    vmem = pl.BlockSpec(memory_space=pltpu.VMEM)
    hbm = pl.BlockSpec(memory_space=pl.ANY)
    dma = pltpu.SemaphoreType.DMA
    picked = pl.pallas_call(
        functools.partial(exchange, near, deep, slab_rows),
        out_shape=jax.ShapeDtypeStruct((wide, slab_rows * deep, probes_here), BF16),
        in_specs=[vmem, vmem, vmem, hbm, hbm],
        out_specs=hbm,
        scratch_shapes=[
            pltpu.VMEM(ctab.shape, BF16),
            pltpu.VMEM(rtab.shape[1:], BF16),
            pltpu.VMEM((chips * 4, lanes), F32),
            pltpu.VMEM((chips, 4, lanes), BF16),
            pltpu.VMEM((chips, 4, lanes), BF16),
            pltpu.VMEM((chips, 4, lanes), BF16),
            pltpu.VMEM((2 * QUAD * SPOTS, kdim), BF16),
            pltpu.VMEM((SPOTS, 8 * lanes), BF16),
            pltpu.VMEM((SPOTS, 8 * lanes), BF16),
            pltpu.VMEM((deep, 2 * slab_rows, LANES), BF16),
            pltpu.VMEM((LANES // 128, 2 * slab_rows * deep, 128), F32),
            pltpu.VMEM((SPOTS, near * probes_here), BF16),
            pltpu.VMEM((near, 8, probes_here), F32),
            pltpu.VMEM((near, 2, slab_rows * deep, probes_here), BF16),
            dma, dma, dma, dma, dma, dma,
            dma((deep,)), dma((deep,)), dma((near,)), dma((near,)),
            dma((near, 2)), dma((wide,)), dma,
        ],
        compiler_params=pltpu.CompilerParams(
            collective_id=0, has_side_effects=True, vmem_limit_bytes=48 * 1024 * 1024
        ),
    )(smatrix.reshape(2, beams_here * slab_rows, cols), beam, spot, ctab, rtab)
    step = min(8, slab_rows)
    return pl.pallas_call(
        functools.partial(to_columns, deep),
        grid=(slab_rows // step,),
        in_specs=[pl.BlockSpec((wide, step * deep, probes_here), lambda i: (0, i, 0))],
        out_specs=pl.BlockSpec((probes_here, step, cols), lambda i: (0, i, 0)),
        out_shape=jax.ShapeDtypeStruct((probes_here, slab_rows, cols), F32),
    )(picked)


def solution(mesh):
    return jax.shard_map(
        on_device,
        mesh=mesh,
        in_specs=(P(None, "probe", "slab", None), P(), P(), P("probe", None)),
        out_specs=P("probe", "slab", None),
        check_vma=False,
    )
```

```python
import functools
import math

import jax
import jax.numpy as jnp
import ml_dtypes
import numpy as np
from jax import lax
from jax.experimental import pallas as pl
from jax.experimental.pallas import tpu as pltpu
from jax.sharding import PartitionSpec as P

HALO = 8
SIDE = 2 * HALO + 1
SPOTS = 304
QUAD = 4
MESH = pl.DeviceIdType.MESH
F32 = jnp.float32
BF16 = jnp.bfloat16


def two_terms(table):
    high = table.astype(ml_dtypes.bfloat16)
    low = (table - high.astype(np.float64)).astype(ml_dtypes.bfloat16)
    return np.stack([high, low])


def column_table(near, deep, cols):
    chip = np.arange(cols)
    far, probe = chip // (near * deep), chip % (near * deep)
    freq = (far * near + probe % near) * deep + probe // near
    turn = 2.0 * np.pi * ((freq[:, None] * np.arange(cols)[None, :]) % cols) / cols
    cos, sin = np.cos(turn), np.sin(turn)
    return two_terms(np.block([[cos, sin], [-sin, cos]]))


def row_table(slab_rows, slabs):
    length = slab_rows * slabs
    tables = []
    for core in range(2):
        freq = np.concatenate(
            [(far * 2 + core) * slab_rows + np.arange(slab_rows) for far in range(2)]
        )
        row = np.concatenate(
            [
                np.tile((far * 2 + side) * slab_rows + np.arange(slab_rows), QUAD)
                for side in (core, 1 - core)
                for far in range(2)
            ]
        )
        turn = 2.0 * np.pi * ((freq[:, None] * row[None, :]) % length) / length
        cos, sin = np.cos(turn), np.sin(turn)
        tables.append(two_terms(np.block([[cos, sin], [-sin, cos]])))
    return np.stack(tables)


def nt(a, b):
    return lax.dot_general(a, b, (((1,), (1,)), ((), ())), preferred_element_type=F32)


def unit_circle(turn):
    turn = turn - jnp.floor(turn + 0.5)
    quarter = jnp.floor(4.0 * turn + 0.5)
    phi = (2.0 * math.pi) * (turn - 0.25 * quarter)
    sq = phi * phi
    s = phi * (1.0 + sq * (-1.0 / 6 + sq * (1.0 / 120 + sq * (-1.0 / 5040 + sq / 362880))))
    c = 1.0 + sq * (-0.5 + sq * (1.0 / 24 + sq * (-1.0 / 720 + sq / 40320)))
    odd = jnp.abs(quarter) == 1.0
    a = jnp.where(odd, s, c)
    b = jnp.where(odd, c, s)
    cos_neg = (quarter == 1.0) | (jnp.abs(quarter) == 2.0)
    sin_neg = (quarter == -1.0) | (jnp.abs(quarter) == 2.0)
    return jnp.where(cos_neg, -a, a), jnp.where(sin_neg, -b, b)


def spot_offsets(width):
    spot = lax.broadcasted_iota(jnp.int32, (SPOTS, width), 0).astype(F32)
    row = jnp.floor((spot + 0.5) * (1.0 / SIDE))
    return row - HALO, spot - SIDE * row - HALO


def beam_rows(amp_ref, freq_ref, probes):
    kdim = 4 * probes
    beams = amp_ref.shape[1]
    rows = [freq_ref[0:1, :].astype(F32), freq_ref[1:2, :].astype(F32)]
    for part in range(2):
        rest = amp_ref[part : part + 1, :]
        for _ in range(3):
            piece = rest.astype(BF16).astype(F32)
            rows.append(piece)
            rest = rest - piece
    stack = jnp.concatenate(rows, axis=0).astype(BF16)
    beam = lax.broadcasted_iota(jnp.int32, (beams, QUAD * kdim), 0)
    lane = lax.broadcasted_iota(jnp.int32, (beams, QUAD * kdim), 1)
    j, k = lane // kdim, lane % kdim
    pick = beam == (k // 4) * 8 + (k % 2) * QUAD + j
    got = jnp.dot(stack, jnp.where(pick, 1.0, 0.0).astype(BF16), preferred_element_type=F32)
    re = got[2:3] + got[3:4] + got[4:5]
    im = got[5:6] + got[6:7] + got[7:8]
    second = (lax.broadcasted_iota(jnp.int32, (1, QUAD * kdim), 1) // 2) % 2 == 1
    return got[0:1], got[1:2], jnp.where(second, -im, re), jnp.where(second, re, im)


def exchange(
    near, deep,
    s_ref, amp_ref, freq_ref, place_ref, ctab_hbm, rtab_hbm, out_ref,
    ctab, rtab, sendf, send, field, other, weight, high, low, planes, picks, spot, spots,
    blocks, landed, wide_f,
    ctab_sem, rtab_sem, send_sem, recv_sem, pair_send, pair_recv,
    deep_send, deep_recv, spot_send, spot_recv, near_send, near_recv,
):
    probe, slab = lax.axis_index("probe"), lax.axis_index("slab")
    _, beams_here, slab_rows, cols = s_ref.shape
    probes = near * deep
    chips = 2 * probes
    wide = 2 * near
    far, core = slab // 2, slab % 2
    chip = far * probes + probe
    z, flat = probe // near, probe % near
    here = far * near + flat

    def device(index):
        return (index % probes, (index // probes) * 2 + core)

    pair = (probe, far * 2 + 1 - core)
    barrier = pltpu.get_barrier_semaphore()

    @pl.loop(1, chips)
    def _(i):
        pl.semaphore_signal(barrier, inc=1, device_id=device((chip + i) % chips), device_id_type=MESH)

    pl.semaphore_signal(barrier, inc=1, device_id=pair, device_id_type=MESH)
    ctab_copy = pltpu.make_async_copy(ctab_hbm, ctab, ctab_sem)
    ctab_copy.start()
    rtab_copy = pltpu.make_async_copy(rtab_hbm.at[core], rtab, rtab_sem)
    rtab_copy.start()
    width = place_ref.shape[1]
    index = (place_ref[0:1, :] + HALO) * SIDE + place_ref[1:2, :] + HALO
    spot[...] = jnp.broadcast_to(index.astype(F32), (8, width))

    ctab_copy.wait()
    parts = [s_ref[part].reshape(beams_here * slab_rows, cols) for part in range(2)]
    both = jnp.concatenate(parts, axis=1)
    half = nt(ctab[0], both) + nt(ctab[1], both)
    lanes = QUAD * slab_rows
    for part in range(2):
        for h in range(2):
            sendf[pl.ds(part * 2 + h, chips, stride=4), :] = half[
                part * chips : (part + 1) * chips, h * lanes : (h + 1) * lanes
            ]
    send[...] = sendf[...].astype(BF16).reshape(chips, 4, lanes)
    spots[flat] = spot[...]
    pl.semaphore_wait(barrier, chips)

    @pl.loop(1, chips)
    def _(i):
        to = (chip + i) % chips
        pltpu.make_async_remote_copy(
            src_ref=send.at[to], dst_ref=field.at[chip], send_sem=send_sem, recv_sem=recv_sem,
            device_id=device(to), device_id_type=MESH,
        ).start()

    pltpu.make_async_copy(send.at[chip], field.at[chip], recv_sem).start()
    spot_copies = []
    for i in range(1, near):
        copy = pltpu.make_async_remote_copy(
            src_ref=spot, dst_ref=spots.at[flat], send_sem=spot_send.at[i],
            recv_sem=spot_recv.at[flat], device_id=(z * near + (flat + i) % near, slab),
            device_id_type=MESH,
        )
        copy.start()
        spot_copies.append(copy)

    kdim = weight.shape[1]
    f0, f1, amp_re, amp_im = beam_rows(amp_ref, freq_ref, probes)
    r0, c0 = spot_offsets(kdim)
    for j in range(QUAD):
        at = slice(j * kdim, (j + 1) * kdim)
        cos, sin = unit_circle((f0[:, at] * r0 + f1[:, at] * c0) * (1.0 / (4 * slab_rows)))
        re, im = amp_re[:, at], amp_im[:, at]
        weight[j * SPOTS : (j + 1) * SPOTS, :] = (re * cos + im * sin).astype(BF16)
        weight[(4 + j) * SPOTS : (5 + j) * SPOTS, :] = (im * cos - re * sin).astype(BF16)

    pltpu.make_async_copy(field, field, recv_sem).wait()
    swap = pltpu.make_async_remote_copy(
        src_ref=field, dst_ref=other, send_sem=pair_send, recv_sem=pair_recv,
        device_id=pair, device_id_type=MESH,
    )
    swap.start()

    def beam_sum(source, side, turn):
        r0, _ = spot_offsets(2 * lanes)
        lane = lax.broadcasted_iota(jnp.int32, (SPOTS, 2 * lanes), 1)
        group = (lane % lanes) // slab_rows
        row = ((lane // lanes) * 2 + side) * slab_rows + lane % slab_rows
        rowf = row.astype(F32)
        inside = (rowf >= r0) & (rowf < r0 + 4.0 * slab_rows)
        x = jnp.concatenate(
            [
                source[0:probes].reshape(probes * 4, lanes),
                source[probes : 2 * probes].reshape(probes * 4, lanes),
            ],
            axis=1,
        )
        for part in range(2):
            total = None
            for j in range(QUAD):
                w = weight[(part * QUAD + j) * SPOTS : (part * QUAD + j + 1) * SPOTS, :]
                y = jnp.dot(w, x, preferred_element_type=F32)
                total = y if j == 0 else jnp.where(group == j, y, total)
            total = jnp.where(inside, total, 0.0)
            top = total.astype(BF16)
            at = (part * 2 + turn) * 2 * lanes
            high[:, at : at + 2 * lanes] = top
            low[:, at : at + 2 * lanes] = (total - top.astype(F32)).astype(BF16)

    beam_sum(field, core, 0)
    for i in range(near):
        at = (flat + i) % near
        if i > 0:
            pltpu.make_async_remote_copy(
                src_ref=spot, dst_ref=spots.at[at], send_sem=spot_send.at[i],
                recv_sem=spot_recv.at[at], device_id=pair, device_id_type=MESH,
            ).wait_recv()
        row = lax.broadcasted_iota(jnp.int32, (384, width), 0)
        row = jnp.where(row >= 320, row - 64, row).astype(F32)
        hit = row == spots[at][0:1, :]
        picks[:, i * width : (i + 1) * width] = jnp.where(hit, 1.0, 0.0).astype(BF16)
    swap.wait_recv()
    beam_sum(other, 1 - core, 1)
    rtab_copy.wait()
    out = nt(rtab[0], high[...]) + (nt(rtab[0], low[...]) + nt(rtab[1], high[...]))
    count = 2 * slab_rows
    re, im = out[:count], out[count:]
    scale = 1.0 / (4 * slab_rows * chips)
    power = ((re * re + im * im) * scale).astype(BF16)
    rest = jnp.concatenate([power[:, 256:SPOTS], jnp.zeros((count, 320 - SPOTS), BF16)], axis=1)
    planes[z, 0:count] = power[:, 0:128]
    planes[z, count : 2 * count] = power[:, 128:256]
    planes[z, 2 * count :] = jnp.concatenate([rest[:slab_rows], rest[slab_rows:]], axis=1)

    def deep_copy(i, slot):
        return pltpu.make_async_remote_copy(
            src_ref=planes.at[slot], dst_ref=planes.at[slot], send_sem=deep_send.at[i],
            recv_sem=deep_recv.at[slot], device_id=(((z + i) % deep) * near + flat, slab),
            device_id_type=MESH,
        )

    def near_copy(i, target, off, slot):
        return pltpu.make_async_remote_copy(
            src_ref=blocks.at[off * wide + i * 2 + target], dst_ref=landed.at[slot],
            send_sem=near_send, recv_sem=near_recv.at[here],
            device_id=(z * near + (flat + i) % near, target * 2 + core), device_id_type=MESH,
        )

    order = sorted(range(1, deep), key=lambda i: (min(i, deep - i), i))
    for i in order:
        deep_copy(i, z).start()
    lane = lax.broadcasted_iota(jnp.int32, (slab_rows, 128), 1)
    stages = [[0]] + [order[i : i + 2] for i in range(0, deep - 1, 2)]
    for stage in stages:
        lefts = []
        for off in stage:
            slot = (z + off) % deep
            if off > 0:
                deep_copy(off, slot).wait_recv()
            block = planes[slot]
            rest = block[2 * count :].astype(F32)
            rest = jnp.concatenate(
                [jnp.where(lane < 64, rest, 0.0), jnp.where(lane >= 64, rest, 0.0)], axis=0
            ).astype(BF16)
            lefts.append(
                jnp.concatenate([block[0:count], block[count : 2 * count], rest], axis=1)
            )
        left = lefts[0] if len(lefts) == 1 else jnp.concatenate(lefts, axis=0)
        got = jnp.dot(left, picks[...], preferred_element_type=F32).astype(BF16)
        for n, off in enumerate(stage):
            for i in range(near):
                for target in range(2):
                    at = n * count + target * slab_rows
                    blocks[off * wide + i * 2 + target] = got[
                        at : at + slab_rows, i * width : (i + 1) * width
                    ]
            slot = here * deep + (z + off) % deep
            near_copy(0, 1 - far, off, slot).start()

            @pl.loop(1, near)
            def _(i):
                near_copy(i, 0, off, slot).start()
                near_copy(i, 1, off, slot).start()

            landed[slot] = blocks[off * wide + far]

    for i in range(wide):
        source = (here + i) % wide
        at = pl.ds(source * deep, deep)
        if i > 0:
            pltpu.make_async_remote_copy(
                src_ref=landed.at[at], dst_ref=landed.at[at], send_sem=near_send,
                recv_sem=near_recv.at[source], device_id=pair, device_id_type=MESH,
            ).wait_recv()
        rows = deep * slab_rows
        wide_f[pl.ds(pl.multiple_of(source * rows, rows), rows), :] = (
            landed[at].astype(F32).reshape(rows, width)
        )
    for k in range(slab_rows):
        out_ref[:, k, :] = wide_f[pl.ds(k, wide * deep, stride=slab_rows), :].T
    for i in order:
        deep_copy(i, z).wait_send()
    for copy in spot_copies:
        copy.wait_send()
    swap.wait_send()
    gone = send.at[pl.ds(0, chips - 1)]
    pltpu.make_async_copy(gone, gone, send_sem).wait()
    gone = blocks.at[pl.ds(0, (wide - 1) * deep)]
    pltpu.make_async_copy(gone, gone, near_send).wait()


def on_device(smatrix, amplitude, beam_index, positions):
    _, beams_here, slab_rows, cols = smatrix.shape
    probes = lax.axis_size("probe")
    near = 8 if probes == 64 else 2
    deep = probes // near
    wide = 2 * near
    chips = 2 * probes
    slabs = lax.axis_size("slab")
    width = positions.shape[0]
    lanes = QUAD * slab_rows
    kdim = 4 * probes
    ctab = jnp.asarray(column_table(near, deep, cols))
    rtab = jnp.asarray(row_table(slab_rows, slabs))
    vmem = pl.BlockSpec(memory_space=pltpu.VMEM)
    hbm = pl.BlockSpec(memory_space=pltpu.HBM)
    dma = pltpu.SemaphoreType.DMA
    return pl.pallas_call(
        functools.partial(exchange, near, deep),
        out_shape=jax.ShapeDtypeStruct((width, slab_rows, cols), F32),
        in_specs=[vmem, vmem, vmem, vmem, hbm, hbm],
        out_specs=vmem,
        scratch_shapes=[
            pltpu.VMEM(ctab.shape, BF16),
            pltpu.VMEM(rtab.shape[1:], BF16),
            pltpu.VMEM((chips * 4, lanes), F32),
            pltpu.VMEM((chips, 4, lanes), BF16),
            pltpu.VMEM((chips, 4, lanes), BF16),
            pltpu.VMEM((chips, 4, lanes), BF16),
            pltpu.VMEM((2 * QUAD * SPOTS, kdim), BF16),
            pltpu.VMEM((SPOTS, 8 * lanes), BF16),
            pltpu.VMEM((SPOTS, 8 * lanes), BF16),
            pltpu.VMEM((deep, 5 * slab_rows, 128), BF16),
            pltpu.VMEM((384, near * width), BF16),
            pltpu.VMEM((8, width), F32),
            pltpu.VMEM((near, 8, width), F32),
            pltpu.VMEM((wide * deep, slab_rows, width), BF16),
            pltpu.VMEM((wide * deep, slab_rows, width), BF16),
            pltpu.VMEM((wide * deep * slab_rows, width), F32),
            dma, dma, dma, dma, dma, dma,
            dma((deep,)), dma((deep,)), dma((near,)), dma((near,)), dma, dma((wide,)),
        ],
        compiler_params=pltpu.CompilerParams(
            collective_id=0, has_side_effects=True, vmem_limit_bytes=48 * 1024 * 1024
        ),
    )(smatrix, amplitude, beam_index.T, positions.T, ctab, rtab)


def solution(mesh):
    return jax.shard_map(
        on_device,
        mesh=mesh,
        in_specs=(P(None, "probe", "slab", None), P(), P(), P("probe", None)),
        out_specs=P("probe", "slab", None),
        check_vma=False,
    )
```

```python
import functools
import math

import jax
import jax.numpy as jnp
import ml_dtypes
import numpy as np
from jax import lax
from jax.experimental import pallas as pl
from jax.experimental.pallas import tpu as pltpu
from jax.sharding import PartitionSpec as P

HALO = 8
SIDE = 2 * HALO + 1
SPOTS = 304
QUAD = 4
MESH = pl.DeviceIdType.MESH
F32 = jnp.float32
BF16 = jnp.bfloat16


def two_terms(table):
    high = table.astype(ml_dtypes.bfloat16)
    low = (table - high.astype(np.float64)).astype(ml_dtypes.bfloat16)
    return np.stack([high, low])


def column_table(near, deep, cols):
    chip = np.arange(cols)
    far, probe = chip // (near * deep), chip % (near * deep)
    freq = (far * near + probe % near) * deep + probe // near
    turn = 2.0 * np.pi * ((freq[:, None] * np.arange(cols)[None, :]) % cols) / cols
    cos, sin = np.cos(turn), np.sin(turn)
    return two_terms(np.block([[cos, sin], [-sin, cos]]))


def row_table(slab_rows, slabs):
    length = slab_rows * slabs
    tables = []
    for core in range(2):
        freq = np.concatenate(
            [(far * 2 + core) * slab_rows + np.arange(slab_rows) for far in range(2)]
        )
        row = np.concatenate(
            [
                (far * 2 + side) * slab_rows + np.arange(slab_rows)
                for side in (core, 1 - core)
                for far in range(2)
            ]
        )
        turn = 2.0 * np.pi * ((freq[:, None] * row[None, :]) % length) / length
        cos, sin = np.cos(turn), np.sin(turn)
        tables.append(two_terms(np.block([[cos, sin], [-sin, cos]])))
    return np.stack(tables)


def nt(a, b):
    return lax.dot_general(a, b, (((1,), (1,)), ((), ())), preferred_element_type=F32)


def unit_circle(turn):
    turn = turn - jnp.floor(turn + 0.5)
    quarter = jnp.floor(4.0 * turn + 0.5)
    phi = (2.0 * math.pi) * (turn - 0.25 * quarter)
    sq = phi * phi
    s = phi * (1.0 + sq * (-1.0 / 6 + sq * (1.0 / 120 + sq * (-1.0 / 5040 + sq / 362880))))
    c = 1.0 + sq * (-0.5 + sq * (1.0 / 24 + sq * (-1.0 / 720 + sq / 40320)))
    odd = jnp.abs(quarter) == 1.0
    a = jnp.where(odd, s, c)
    b = jnp.where(odd, c, s)
    cos_neg = (quarter == 1.0) | (jnp.abs(quarter) == 2.0)
    sin_neg = (quarter == -1.0) | (jnp.abs(quarter) == 2.0)
    return jnp.where(cos_neg, -a, a), jnp.where(sin_neg, -b, b)


def spot_offsets(width):
    spot = lax.broadcasted_iota(jnp.int32, (SPOTS, width), 0).astype(F32)
    row = jnp.floor((spot + 0.5) * (1.0 / SIDE))
    return row - HALO, spot - SIDE * row - HALO


def beam_rows(amp_ref, freq_ref, probes):
    kdim = 4 * probes
    beams = amp_ref.shape[1]
    rows = [freq_ref[0:1, :].astype(F32), freq_ref[1:2, :].astype(F32)]
    for part in range(2):
        rest = amp_ref[part : part + 1, :]
        for _ in range(3):
            piece = rest.astype(BF16).astype(F32)
            rows.append(piece)
            rest = rest - piece
    stack = jnp.concatenate(rows, axis=0).astype(BF16)
    beam = lax.broadcasted_iota(jnp.int32, (beams, QUAD * kdim), 0)
    lane = lax.broadcasted_iota(jnp.int32, (beams, QUAD * kdim), 1)
    j, k = lane // kdim, lane % kdim
    pick = beam == (k // 4) * 8 + (k % 2) * QUAD + j
    got = jnp.dot(stack, jnp.where(pick, 1.0, 0.0).astype(BF16), preferred_element_type=F32)
    re = got[2:3] + got[3:4] + got[4:5]
    im = got[5:6] + got[6:7] + got[7:8]
    second = (lax.broadcasted_iota(jnp.int32, (1, QUAD * kdim), 1) // 2) % 2 == 1
    return got[0:1], got[1:2], jnp.where(second, -im, re), jnp.where(second, re, im)


def exchange(
    near, deep,
    s_hbm, amp_hbm, freq_hbm, place_hbm, ctab_hbm, rtab_hbm, out_ref,
    s_ref, amp_ref, freq_ref, place_ref, ctab, rtab, sendf, send, field, other, beams_f, weight, planes, picks, spot, spots,
    blocks, landed, wide_f,
    s_sem, amp_sem, freq_sem, place_sem, ctab_sem, rtab_sem, send_sem, recv_sem, pair_send, pair_recv,
    deep_send, deep_recv, spot_send, spot_recv, near_send, near_recv,
):
    probe, slab = lax.axis_index("probe"), lax.axis_index("slab")
    _, beams_here, slab_rows, cols = s_ref.shape
    probes = near * deep
    chips = 2 * probes
    wide = 2 * near
    far, core = slab // 2, slab % 2
    chip = far * probes + probe
    z, flat = probe // near, probe % near
    here = far * near + flat

    def device(index):
        return (index % probes, (index // probes) * 2 + core)

    pair = (probe, far * 2 + 1 - core)
    barrier = pltpu.get_barrier_semaphore()

    def others(body):
        for dz in sorted(range(deep), key=lambda i: -min(i, deep - i)):

            @pl.loop(0 if dz else 1, wide)
            def _(e):
                at = (here + e) % wide
                body((at // near) * probes + ((z + dz) % deep) * near + at % near)

    others(
        lambda to: pl.semaphore_signal(
            barrier, inc=1, device_id=device(to), device_id_type=MESH
        )
    )
    pl.semaphore_signal(barrier, inc=1, device_id=pair, device_id_type=MESH)
    s_copy = pltpu.make_async_copy(s_hbm, s_ref, s_sem)
    ctab_copy = pltpu.make_async_copy(ctab_hbm, ctab, ctab_sem)
    place_copy = pltpu.make_async_copy(place_hbm, place_ref, place_sem)
    amp_copy = pltpu.make_async_copy(amp_hbm, amp_ref, amp_sem)
    freq_copy = pltpu.make_async_copy(freq_hbm, freq_ref, freq_sem)
    rtab_copy = pltpu.make_async_copy(rtab_hbm.at[core], rtab, rtab_sem)
    for copy in (s_copy, ctab_copy, place_copy, amp_copy, freq_copy, rtab_copy):
        copy.start()
    place_copy.wait()
    width = place_ref.shape[1]
    index = (place_ref[0:1, :] + HALO) * SIDE + place_ref[1:2, :] + HALO
    spot[...] = jnp.broadcast_to(index.astype(F32), (8, width))

    s_copy.wait()
    ctab_copy.wait()
    parts = [s_ref[part].reshape(beams_here * slab_rows, cols) for part in range(2)]
    both = jnp.concatenate(parts, axis=1)
    half = nt(ctab[0], both) + nt(ctab[1], both)
    lanes = QUAD * slab_rows
    for part in range(2):
        for h in range(2):
            sendf[pl.ds(part * 2 + h, chips, stride=4), :] = half[
                part * chips : (part + 1) * chips, h * lanes : (h + 1) * lanes
            ]
    send[...] = sendf[...].astype(BF16).reshape(chips, 4, lanes)
    spots[flat] = spot[...]
    pl.semaphore_wait(barrier, chips)

    others(
        lambda to: pltpu.make_async_remote_copy(
            src_ref=send.at[to], dst_ref=field.at[chip], send_sem=send_sem, recv_sem=recv_sem,
            device_id=device(to), device_id_type=MESH,
        ).start()
    )
    pltpu.make_async_copy(send.at[chip], field.at[chip], recv_sem).start()
    spot_copies = []
    for i in range(1, near):
        copy = pltpu.make_async_remote_copy(
            src_ref=spot, dst_ref=spots.at[flat], send_sem=spot_send.at[i],
            recv_sem=spot_recv.at[flat], device_id=(z * near + (flat + i) % near, slab),
            device_id_type=MESH,
        )
        copy.start()
        spot_copies.append(copy)

    amp_copy.wait()
    freq_copy.wait()
    kdim = 4 * probes
    f0, f1, amp_re, amp_im = beam_rows(amp_ref, freq_ref, probes)
    r0, c0 = spot_offsets(kdim)
    for j in range(QUAD):
        at = slice(j * kdim, (j + 1) * kdim)
        cos, sin = unit_circle((f0[:, at] * r0 + f1[:, at] * c0) * (1.0 / (4 * slab_rows)))
        re, im = amp_re[:, at], amp_im[:, at]
        weight[0:SPOTS, at] = (re * cos + im * sin).astype(BF16)
        weight[SPOTS:, at] = (im * cos - re * sin).astype(BF16)
    for i in range(near):
        at = (flat + i) % near
        if i > 0:
            pltpu.make_async_remote_copy(
                src_ref=spot, dst_ref=spots.at[at], send_sem=spot_send.at[i],
                recv_sem=spot_recv.at[at], device_id=pair, device_id_type=MESH,
            ).wait_recv()
        row = lax.broadcasted_iota(jnp.int32, (384, width), 0)
        row = jnp.where(row >= 320, row - 64, row).astype(F32)
        hit = row == spots[at][0:1, :]
        picks[:, i * width : (i + 1) * width] = jnp.where(hit, 1.0, 0.0).astype(BF16)

    pltpu.make_async_copy(field, field, recv_sem).wait()
    swap = pltpu.make_async_remote_copy(
        src_ref=field, dst_ref=other, send_sem=pair_send, recv_sem=pair_recv,
        device_id=pair, device_id_type=MESH,
    )
    swap.start()

    group = lax.broadcasted_iota(jnp.int32, (kdim, lanes), 1) // slab_rows

    def spread(source, turn):
        for far_of in range(2):
            t = turn * 2 + far_of
            x = source[far_of * probes : (far_of + 1) * probes].reshape(kdim, lanes).astype(F32)
            for j in range(QUAD):
                shift = ((t - j) % QUAD) * slab_rows
                moved = pltpu.roll(x, shift, 1) if shift else x
                at = slice(j * kdim, (j + 1) * kdim)
                sofar = moved if t == 0 else jnp.where(group == t, moved, beams_f[at, :])
                beams_f[at, :] = sofar

    spread(field, 0)
    swap.wait_recv()
    spread(other, 1)
    total = jnp.dot(weight[...], beams_f[...].astype(BF16), preferred_element_type=F32)
    r0, _ = spot_offsets(lanes)
    lane = lax.broadcasted_iota(jnp.int32, (SPOTS, lanes), 1)
    t = lane // slab_rows
    side = jnp.where(t < 2, core, 1 - core)
    row = (((t % 2) * 2 + side) * slab_rows + lane % slab_rows).astype(F32)
    inside = (row >= r0) & (row < r0 + 4.0 * slab_rows)
    both = jnp.concatenate(
        [jnp.where(inside, total[0:SPOTS], 0.0), jnp.where(inside, total[SPOTS:], 0.0)], axis=1
    )
    high = both.astype(BF16)
    low = (both - high.astype(F32)).astype(BF16)
    rtab_copy.wait()
    out = nt(rtab[0], high) + (nt(rtab[0], low) + nt(rtab[1], high))
    count = 2 * slab_rows
    re, im = out[:count], out[count:]
    scale = 1.0 / (4 * slab_rows * chips)
    power = ((re * re + im * im) * scale).astype(BF16)
    rest = jnp.concatenate([power[:, 256:SPOTS], jnp.zeros((count, 320 - SPOTS), BF16)], axis=1)
    planes[z, 0:count] = power[:, 0:128]
    planes[z, count : 2 * count] = power[:, 128:256]
    planes[z, 2 * count :] = jnp.concatenate([rest[:slab_rows], rest[slab_rows:]], axis=1)

    def deep_copy(i, slot, send_at, recv_at, rows=slice(None)):
        return pltpu.make_async_remote_copy(
            src_ref=planes.at[slot, rows], dst_ref=planes.at[slot, rows],
            send_sem=deep_send.at[send_at], recv_sem=deep_recv.at[recv_at],
            device_id=(((z + i) % deep) * near + flat, slab), device_id_type=MESH,
        )

    def near_copy(i, target, off, slot):
        return pltpu.make_async_remote_copy(
            src_ref=blocks.at[off * wide + i * 2 + target], dst_ref=landed.at[slot],
            send_sem=near_send, recv_sem=near_recv.at[here],
            device_id=(z * near + (flat + i) % near, target * 2 + core), device_id_type=MESH,
        )

    lane = lax.broadcasted_iota(jnp.int32, (slab_rows, 128), 1)

    def pick_and_send(stage):
        lefts = []
        for off in stage:
            block = planes[(z + off) % deep]
            rest = block[2 * count :].astype(F32)
            rest = jnp.concatenate(
                [jnp.where(lane < 64, rest, 0.0), jnp.where(lane >= 64, rest, 0.0)], axis=0
            ).astype(BF16)
            lefts.append(
                jnp.concatenate([block[0:count], block[count : 2 * count], rest], axis=1)
            )
        left = lefts[0] if len(lefts) == 1 else jnp.concatenate(lefts, axis=0)
        got = jnp.dot(left, picks[...], preferred_element_type=F32).astype(BF16)
        for n, off in enumerate(stage):
            for i in range(near):
                for target in range(2):
                    at = n * count + target * slab_rows
                    blocks[off * wide + i * 2 + target] = got[
                        at : at + slab_rows, i * width : (i + 1) * width
                    ]
            slot = here * deep + (z + off) % deep
            near_copy(0, 1 - far, off, slot).start()

            @pl.loop(1, near)
            def _(i):
                near_copy(i, 0, off, slot).start()
                near_copy(i, 1, off, slot).start()

            landed[slot] = blocks[off * wide + far]

    def arrived(off, recv_at=None, rows=slice(None)):
        slot = (z + off) % deep
        deep_copy(off, slot, 0, slot if recv_at is None else recv_at, rows).wait_recv()

    sent = []

    def pass_on(i, off, recv_at=None, rows=slice(None)):
        slot = (z + off) % deep
        copy = deep_copy(i, slot, len(sent), slot if recv_at is None else recv_at, rows)
        copy.start()
        sent.append(copy)

    if deep == 8:
        first, second = slice(0, 80), slice(80, 160)
        for i in (1, 7, 2, 6):
            pass_on(i, 0)
        pick_and_send([0])
        arrived(1)
        arrived(7)
        pick_and_send([1, 7])
        arrived(2)
        arrived(6)
        pass_on(7, 2)
        pass_on(1, 6)
        pass_on(2, 6, None, first)
        pass_on(6, 2, deep, second)
        pick_and_send([2, 6])
        arrived(3)
        arrived(5)
        pick_and_send([3, 5])
        arrived(4, None, first)
        arrived(4, deep, second)
        pick_and_send([4])
    else:
        for i in range(1, deep):
            pass_on(i, 0)
        pick_and_send([0])
        for i in range(1, deep):
            arrived(i)
            pick_and_send([i])

    for i in range(wide):
        source = (here + i) % wide
        at = pl.ds(source * deep, deep)
        if i > 0:
            pltpu.make_async_remote_copy(
                src_ref=landed.at[at], dst_ref=landed.at[at], send_sem=near_send,
                recv_sem=near_recv.at[source], device_id=pair, device_id_type=MESH,
            ).wait_recv()
        rows = deep * slab_rows
        wide_f[pl.ds(pl.multiple_of(source * rows, rows), rows), :] = (
            landed[at].astype(F32).reshape(rows, width)
        )
    for k in range(slab_rows):
        out_ref[:, k, :] = wide_f[pl.ds(k, wide * deep, stride=slab_rows), :].T
    for copy in sent + spot_copies:
        copy.wait_send()
    swap.wait_send()
    gone = send.at[pl.ds(0, chips - 1)]
    pltpu.make_async_copy(gone, gone, send_sem).wait()
    gone = blocks.at[pl.ds(0, (wide - 1) * deep)]
    pltpu.make_async_copy(gone, gone, near_send).wait()


def on_device(smatrix, amplitude, beam_index, positions):
    _, beams_here, slab_rows, cols = smatrix.shape
    probes = lax.axis_size("probe")
    near = max(1, probes // 8)
    deep = probes // near
    wide = 2 * near
    chips = 2 * probes
    slabs = lax.axis_size("slab")
    width = positions.shape[0]
    lanes = QUAD * slab_rows
    kdim = 4 * probes
    ctab = jnp.asarray(column_table(near, deep, cols))
    rtab = jnp.asarray(row_table(slab_rows, slabs))
    operands = (smatrix, amplitude, beam_index.T, positions.T, ctab, rtab)
    vmem = pl.BlockSpec(memory_space=pltpu.VMEM)
    hbm = pl.BlockSpec(memory_space=pltpu.HBM)
    dma = pltpu.SemaphoreType.DMA
    return pl.pallas_call(
        functools.partial(exchange, near, deep),
        out_shape=jax.ShapeDtypeStruct((width, slab_rows, cols), F32),
        in_specs=[hbm] * 6,
        out_specs=vmem,
        scratch_shapes=[
            pltpu.VMEM(smatrix.shape, BF16),
            pltpu.VMEM(amplitude.shape, F32),
            pltpu.VMEM((2, amplitude.shape[1]), jnp.int32),
            pltpu.VMEM((2, width), jnp.int32),
            pltpu.VMEM(ctab.shape, BF16),
            pltpu.VMEM(rtab.shape[1:], BF16),
            pltpu.VMEM((chips * 4, lanes), F32),
            pltpu.VMEM((chips, 4, lanes), BF16),
            pltpu.VMEM((chips, 4, lanes), BF16),
            pltpu.VMEM((chips, 4, lanes), BF16),
            pltpu.VMEM((QUAD * kdim, lanes), F32),
            pltpu.VMEM((2 * SPOTS, QUAD * kdim), BF16),
            pltpu.VMEM((deep, 5 * slab_rows, 128), BF16),
            pltpu.VMEM((384, near * width), BF16),
            pltpu.VMEM((8, width), F32),
            pltpu.VMEM((near, 8, width), F32),
            pltpu.VMEM((wide * deep, slab_rows, width), BF16),
            pltpu.VMEM((wide * deep, slab_rows, width), BF16),
            pltpu.VMEM((wide * deep * slab_rows, width), F32),
            dma, dma, dma, dma, dma, dma, dma, dma, dma, dma,
            dma((deep,)), dma((deep + 1,)), dma((near,)), dma((near,)), dma, dma((wide,)),
        ],
        compiler_params=pltpu.CompilerParams(
            collective_id=0, has_side_effects=True, vmem_limit_bytes=48 * 1024 * 1024
        ),
    )(*[pltpu.with_memory_space_constraint(v, pltpu.HBM) for v in operands])


def solution(mesh):
    return jax.shard_map(
        on_device,
        mesh=mesh,
        in_specs=(P(None, "probe", "slab", None), P(), P(), P("probe", None)),
        out_specs=P("probe", "slab", None),
        check_vma=False,
    )
```
